32 devices in a mesh: ord: 8 (over y, x, core), ch: 4 (over z).
Axes of the slice: x: 2, y: 2, z: 4, core: 2. Of those that a mesh axis runs over, the one named last changes fastest.
Arguments:
- field_grid: bfloat16 [2, 64, 2, 352, 1440], P(None, 'ch', None, 'ord'), may hold values from -40 to 40
- norm_gain: float32 [64], P('ch'), may hold values from 0.1 to 1.9
- norm_bias: float32 [64], P('ch'), may hold values from -3 to 3
- order_table: int32 [512], replicated, may hold values from 0 to 511, as said below
- legendre: bfloat16 [512, 2, 352, 360], P(('ord', 'ch')), may hold values from -0.3125 to 0.3125
Outputs:
- coefficients: bfloat16 [512, 2, 2, 2, 64, 360], P(('ord', 'ch'))
The draws below stay inside these ranges and needn't reach their ends.
Inputs may be any that keep to these rules, and one draw needn't show every extreme that they name: `order_table`: a permutation of the orders in which slots 2 q and 2 q + 1 hold orders p and 511 - p.
All inputs are finite; a program needn't handle non-finite values.
Results may differ from the reference program's by a relative error of at most 0.0062.
Values may be sent and summed in bfloat16 or wider, within the bound.
A program may use at most 128 MiB of HBM per device.

```python
import math
import jax
import jax.numpy as jnp
from jax import lax

B = 2
C = 64
NH = 352
NLON = 1440
M = 512
LH = 360


def draw_field_grid(key, part):
    keys = jax.random.split(key, 3)
    cycles = jnp.arange(NH, dtype=jnp.float32) / NH
    rising = (1.0 + 2.0 * cycles)[None, None, None, :, None]
    drift = (1.0 + cycles)[None, None, None, :, None]
    channel_scale = jnp.exp(jax.random.uniform(keys[1], (1, C, 1, 1, 1), minval=-0.7, maxval=0.7))
    offsets = jax.random.uniform(keys[2], (B, C, 1, 1, 1), minval=0.2, maxval=0.8)
    noise = jax.random.normal(keys[0], (B, C, 2, NH, NLON), jnp.float32)
    values = channel_scale * (rising * noise + offsets * drift)
    return jnp.clip(values, -40.0, 40.0).astype(jnp.bfloat16)


def draw_order_table(key, part):
    paired = jax.random.permutation(key, M // 2).astype(jnp.int32)
    return jnp.stack([paired, M - 1 - paired], axis=1).reshape(M)


def block_levels(key, extent, cuts, low, top_value):
    level = 1.0
    for axis_at, shards_of in cuts:
        steps = jax.random.uniform(jax.random.fold_in(jax.random.fold_in(key, 6), axis_at), (shards_of,), jnp.float32, low / len(cuts), top_value / len(cuts))
        level = level * jnp.repeat(jnp.exp(steps), extent[axis_at] // shards_of).reshape((-1,) + (1,) * (len(extent) - 1 - axis_at))
    return level


def normal_values(stream_key, dims, scale, limit, cuts=(), kind=jnp.bfloat16):
    factor_of = block_levels(stream_key, dims, cuts, -0.22, 0.18) if cuts else 1.0
    entries = jax.random.normal(stream_key, dims, jnp.float32) * scale * factor_of
    return jnp.minimum(jnp.maximum(entries, -limit), limit).astype(kind)


def setup_inputs(seed: int = 0) -> dict:
    seeds = jax.random.split(jax.random.key(seed), 6)
    return {
        "field_grid": draw_field_grid(jax.random.fold_in(seeds[5], 71), 0),
        "norm_gain": jnp.clip(1.0 + 0.18 * jax.random.normal(seeds[1], (C,), jnp.float32), 0.1, 1.9),
        "norm_bias": normal_values(seeds[2], (C,), 0.5, 3.0, ((0, 4),), jnp.float32),
        "order_table": draw_order_table(jax.random.fold_in(seeds[5], 71), 0),
        "legendre": normal_values(seeds[4], (M, 2, NH, LH), NH ** -0.5, 0.3125, ((0, 32),)),
    }


def fourier_table(orders, length):
    sample = jnp.arange(length, dtype=jnp.int32)
    phases = sample[:, None] * orders[None, :].astype(jnp.int32) % length
    angles = phases.astype(jnp.float32) * (2.0 * math.pi / length)
    factor = 1.0 / math.sqrt(length)
    return jnp.concatenate([jnp.cos(angles) * factor, -jnp.sin(angles) * factor], axis=1).astype(jnp.bfloat16)

def legendre_sums(halves_group, legendre_group, orders_group):
    odd_order = orders_group % 2 == 1
    swapped = jnp.where(odd_order[None, None, None, None, None, :], halves_group[:, :, ::-1], halves_group)
    raw_sums = jnp.einsum('bcpirs,spij->sprbcj', swapped.astype(jnp.float32), legendre_group.astype(jnp.float32))
    degree = 2 * jnp.arange(LH, dtype=jnp.int32)[None, :] + jnp.arange(2, dtype=jnp.int32)[:, None]
    allowed = degree[None, :, :] >= orders_group[:, None, None]
    return jnp.where(allowed[:, :, None, None, None, :], raw_sums, 0.0).astype(jnp.bfloat16)

def reference(field_grid, norm_gain, norm_bias, order_table, legendre):
    values = field_grid.astype(jnp.float32)
    average = lax.optimization_barrier(jnp.mean(values, axis=(2, 3, 4), keepdims=True))
    centered = values - average
    spread = lax.optimization_barrier(jnp.mean(centered * centered, axis=(2, 3, 4), keepdims=True))
    normed = (centered * lax.rsqrt(spread + 1e-05) * norm_gain.reshape(1, C, 1, 1, 1) + norm_bias.reshape(1, C, 1, 1, 1)).astype(jnp.bfloat16)
    twiddle = fourier_table(order_table, NLON)
    fourier = jnp.dot(normed.reshape(-1, NLON), twiddle, preferred_element_type=jnp.float32).reshape(B, C, 2, NH, 2, M)
    halves = jnp.stack([fourier[:, :, 0] + fourier[:, :, 1], fourier[:, :, 0] - fourier[:, :, 1]], axis=2).astype(jnp.bfloat16)
    group_width = 16
    group_count = M // group_width
    halves_grouped = jnp.moveaxis(halves.reshape(B, C, 2, NH, 2, group_count, group_width), 5, 0)
    legendre_grouped = legendre.reshape(group_count, group_width, 2, NH, LH)
    orders_grouped = order_table.reshape(group_count, group_width)

    def one_group(pieces):
        return legendre_sums(pieces[0], pieces[1], pieces[2])
    result = lax.map(one_group, (halves_grouped, legendre_grouped, orders_grouped))
    return result.reshape(M, 2, 2, B, C, LH)
```

```python
from functools import partial
import math

import jax
import jax.numpy as jnp
from jax import lax
from jax.experimental import pallas as pl
from jax.experimental.pallas import tpu as pltpu
from jax.sharding import PartitionSpec as P

MESH = pl.DeviceIdType.MESH
LANES = 128
GROUP = 128
QUAD = 4


def slot_table(orders, length):
    sample = jnp.arange(length, dtype=jnp.int32)
    phases = sample[:, None] * orders[None, :] % length
    angles = phases.astype(jnp.float32) * (2.0 * math.pi / length)
    factor = 1.0 / math.sqrt(length)
    stacked = jnp.stack([jnp.cos(angles) * factor, -jnp.sin(angles) * factor], axis=2)
    return stacked.reshape(length, 2 * orders.shape[0]).astype(jnp.bfloat16)


def legendre_sums(arrived, legendre, orders):
    odd_order = orders % 2 == 1
    swapped = jnp.where(
        odd_order[:, None, None, None, None, None], arrived[:, :, :, :, ::-1], arrived
    )
    raw_sums = jnp.einsum(
        "srbcpi,spij->sprbcj", swapped, legendre, preferred_element_type=jnp.float32
    )
    half_degrees = legendre.shape[3]
    degree = (
        2 * jnp.arange(half_degrees, dtype=jnp.int32)[None, :]
        + jnp.arange(2, dtype=jnp.int32)[:, None]
    )
    allowed = degree[None, :, :] >= orders[:, None, None]
    return jnp.where(allowed[:, :, None, None, None, :], raw_sums, 0.0).astype(jnp.bfloat16)


def general_path(field_grid, norm_gain, norm_bias, order_table, legendre):
    batch_size, chan_local, hemis, cycle_local, longitudes = field_grid.shape
    order_total = order_table.shape[0]
    values = field_grid.astype(jnp.float32)
    cell_count = hemis * cycle_local * lax.axis_size("ord") * longitudes
    partial_sum = jnp.sum(values, axis=(2, 3, 4))
    totals, squares = lax.psum((partial_sum, jnp.sum(values * values, axis=(2, 3, 4))), "ord")
    average = totals / cell_count
    spread = squares / cell_count - average * average
    centered = values - average[:, :, None, None, None]
    inverse_scale = lax.rsqrt(spread + 1e-05) * norm_gain[None, :]
    normed = (
        centered * inverse_scale[:, :, None, None, None] + norm_bias[None, :, None, None, None]
    ).astype(jnp.bfloat16)
    twiddle = slot_table(order_table, longitudes)
    flat_rows = normed.reshape(-1, longitudes)
    fourier = lax.dot_general(
        twiddle, flat_rows, (((0,), (1,)), ((), ())), preferred_element_type=jnp.float32
    )
    fourier = fourier.reshape(order_total, 2, batch_size, chan_local, hemis, cycle_local)
    north = fourier[:, :, :, :, 0]
    south = fourier[:, :, :, :, 1]
    halves = jnp.stack([north + south, north - south], axis=4).astype(jnp.bfloat16)
    slot_count = legendre.shape[0]
    channel_groups = lax.axis_size("ch")
    first_slot = (lax.axis_index("ord") * channel_groups + lax.axis_index("ch")) * slot_count
    own_orders = lax.dynamic_slice_in_dim(order_table, first_slot, slot_count)
    transform = partial(legendre_sums, legendre=legendre, orders=own_orders)
    arrived = lax.all_to_all(
        lax.all_to_all(halves, "ord", split_axis=0, concat_axis=5, tiled=True),
        "ch",
        split_axis=0,
        concat_axis=3,
        tiled=True,
    )
    return transform(arrived)


def angle_tables(orders, length):
    factor = 1.0 / math.sqrt(length)
    step = 2.0 * math.pi / length
    fine = orders[:, None] * jnp.arange(LANES, dtype=jnp.int32)[None, :] % length
    coarse = orders[:, None] * (LANES * jnp.arange(LANES, dtype=jnp.int32))[None, :] % length
    fine = fine.astype(jnp.float32) * step
    coarse = coarse.astype(jnp.float32) * step
    return jnp.stack([jnp.cos(fine) * factor, jnp.sin(fine) * factor, jnp.cos(coarse), jnp.sin(coarse)])


def exchange_kernel(
    sizes, field, tables, signs, gain, bias, out,
    grid, rows, packed, twiddle, sending, stats, stats_in, norms,
    field_sem, stats_out_sem, stats_in_sem, send_sem, recv_sem, own_sem,
):
    n_ord, n_ch, cell_count = sizes
    total = n_ord * n_ch
    fields, hemis, cycles, length = grid.shape
    groups = twiddle.shape[0]
    steps = sending.shape[1]
    tiles = rows.shape[1]
    own_ord, own_ch = lax.axis_index("ord"), lax.axis_index("ch")
    me = own_ord * n_ch + own_ch
    parts = field_sem.shape[0]
    per_part = fields // parts

    def load(part):
        span = pl.ds(part * per_part, per_part)
        return pltpu.make_async_copy(field.at[span], grid.at[span], field_sem.at[part])

    for part in range(parts):
        load(part).start()

    barrier = pltpu.get_barrier_semaphore()

    def greet(hop, carry):
        peer = lax.rem(me + hop, total)
        pl.semaphore_signal(
            barrier, inc=1, device_id=(peer // n_ch, lax.rem(peer, n_ch)), device_id_type=MESH
        )
        return carry

    lax.fori_loop(1, total, greet, 0)

    def fold(values):
        summed = values[:, :LANES]
        for tile in range(1, tiles - 1):
            summed += values[:, tile * LANES : (tile + 1) * LANES]
        rest = values[:, (tiles - 1) * LANES :]
        blank = jnp.zeros((1, LANES - rest.shape[1]), jnp.float32)
        return summed + jnp.concatenate([rest, blank], axis=1)

    for part in range(parts):
        load(part).wait()

        def measure(at, carry, part=part):
            row = part * per_part + at
            first = grid[row, 0].astype(jnp.float32)
            second = grid[row, 1].astype(jnp.float32)
            stats[pl.ds(row, 1), :] = fold(jnp.sum(first + second, axis=0, keepdims=True))
            stats[pl.ds(fields + row, 1), :] = fold(
                jnp.sum(first * first + second * second, axis=0, keepdims=True)
            )
            return carry

        lax.fori_loop(0, per_part, measure, 0)

    pl.semaphore_wait(barrier, total - 1)

    def stats_copy(hop):
        peer = lax.rem(own_ord + hop, n_ord)
        return pltpu.make_async_remote_copy(
            src_ref=stats,
            dst_ref=stats_in.at[own_ord],
            send_sem=stats_out_sem.at[hop],
            recv_sem=stats_in_sem.at[own_ord],
            device_id=(peer, own_ch),
            device_id_type=MESH,
        )

    for hop in range(1, n_ord):
        stats_copy(hop).start()
    stats_in[own_ord] = stats[...]

    def build(group, carry):
        span = pl.ds(pl.multiple_of(group * GROUP, GROUP), GROUP)
        cos_fine, sin_fine = tables[0, span, :], tables[1, span, :]
        cos_coarse, sin_coarse = tables[2, span, :], tables[3, span, :]
        for tile in range(tiles):
            columns = slice(tile * LANES, (tile + 1) * LANES)
            cos_at, sin_at = cos_coarse[:, tile : tile + 1], sin_coarse[:, tile : tile + 1]
            twiddle[group, :GROUP, columns] = (cos_at * cos_fine - sin_at * sin_fine).astype(jnp.bfloat16)
            twiddle[group, GROUP:, columns] = (-(sin_at * cos_fine + cos_at * sin_fine)).astype(jnp.bfloat16)
        return carry

    lax.fori_loop(0, groups, build, 0)

    for hop in range(1, n_ord):
        peer = lax.rem(own_ord + hop, n_ord)
        pltpu.make_async_remote_copy(
            src_ref=stats, dst_ref=stats_in.at[peer], send_sem=stats_out_sem.at[hop],
            recv_sem=stats_in_sem.at[peer], device_id=(peer, own_ch), device_id_type=MESH,
        ).wait()

    merged = stats_in[0]
    for source in range(1, n_ord):
        merged = merged + stats_in[source]
    merged = jnp.sum(merged, axis=1, keepdims=True)
    average = merged[:fields] / cell_count
    spread = merged[fields:] / cell_count - average * average
    scale = lax.rsqrt(spread + 1e-05) * gain[:, :1]
    norms[0] = jnp.broadcast_to(average, (fields, LANES))
    norms[1] = jnp.broadcast_to(scale, (fields, LANES))
    norms[2] = bias[...]

    def normalize(at, carry):
        shift = norms[0, pl.ds(at, 1), :]
        factor = norms[1, pl.ds(at, 1), :]
        offset = norms[2, pl.ds(at, 1), :]
        for hemi in range(hemis):
            for tile in range(tiles):
                piece = grid[at, hemi, :, tile * LANES : min((tile + 1) * LANES, length)]
                wide = piece.shape[1]
                piece = (piece.astype(jnp.float32) - shift[:, :wide]) * factor[:, :wide] + offset[:, :wide]
                if wide < LANES:
                    piece = jnp.concatenate(
                        [piece, jnp.zeros((cycles, LANES - wide), jnp.float32)], axis=1
                    )
                rows[hemi, tile, pl.ds(at, cycles, stride=fields), :] = piece
        return carry

    lax.fori_loop(0, fields, normalize, 0)

    lane = lax.broadcasted_iota(jnp.int32, (GROUP, LANES), 1)
    low = lane // fields % 2 == 0
    high = lane // (2 * fields) % 2 == 0

    def swap(mask, upper, lower, amount):
        return (
            jnp.where(mask, upper, pltpu.roll(lower, amount, 1)),
            jnp.where(mask, pltpu.roll(upper, LANES - amount, 1), lower),
        )

    def advance(step, carry):
        span = pl.ds(pl.multiple_of(step * LANES, LANES), LANES)
        for hemi in range(hemis):
            for tile in range(tiles):
                packed[hemi * LANES : (hemi + 1) * LANES, tile * LANES : (tile + 1) * LANES] = rows[
                    hemi, tile, span, :
                ].astype(jnp.bfloat16)

        def transform(group, inner):
            spectrum = lax.dot_general(
                twiddle[group], packed[...], (((1,), (1,)), ((), ())),
                preferred_element_type=jnp.float32,
            )
            north, south = spectrum[:, :LANES], spectrum[:, LANES:] * signs[group]
            even, odd = north + south, north - south
            a, b, c, d = even[:GROUP], even[GROUP:], odd[:GROUP], odd[GROUP:]
            a, b = swap(low, a, b, fields)
            c, d = swap(low, c, d, fields)
            a, c = swap(high, a, c, 2 * fields)
            b, d = swap(high, b, d, 2 * fields)
            each = GROUP // sending.shape[3]
            for at, piece in enumerate((a, b, c, d)):
                sending[pl.ds(group * each, each), step, at] = piece.astype(jnp.bfloat16).reshape(
                    each, GROUP // each, LANES
                )
            return inner

        lax.fori_loop(0, groups, transform, 0)

        def send(hop, inner):
            peer = lax.rem(me + hop, total)
            pltpu.make_async_remote_copy(
                src_ref=sending.at[peer, step],
                dst_ref=out.at[own_ch, own_ord, step],
                send_sem=send_sem.at[peer],
                recv_sem=recv_sem.at[me],
                device_id=(peer // n_ch, lax.rem(peer, n_ch)),
                device_id_type=MESH,
            ).start()
            return inner

        lax.fori_loop(1, total, send, 0)
        return carry

    lax.fori_loop(0, steps, advance, 0)
    own = pltpu.make_async_copy(sending.at[me], out.at[own_ch, own_ord], own_sem)
    own.start()

    def finish(hop, carry):
        peer = lax.rem(me + hop, total)
        pltpu.make_async_remote_copy(
            src_ref=sending.at[peer],
            dst_ref=out.at[lax.rem(peer, n_ch), peer // n_ch],
            send_sem=send_sem.at[peer],
            recv_sem=recv_sem.at[peer],
            device_id=(peer // n_ch, lax.rem(peer, n_ch)),
            device_id_type=MESH,
        ).wait()
        return carry

    lax.fori_loop(1, total, finish, 0)
    own.wait()


def legendre_kernel(orders, arrived, legendre, out, wide):
    slot = pl.program_id(0)
    sources, depth, lanes = wide.shape
    slots = orders.shape[0]
    cycles = depth // slots

    @pl.when(slot == 0)
    def _():
        for source in range(sources):
            wide[source] = arrived[source].astype(jnp.float32)

    half = lanes // 2
    turned = [
        wide[source, pl.ds(slot, cycles, stride=slots), :].T.astype(jnp.bfloat16)
        for source in range(sources)
    ]
    batch, local = out.shape[3], out.shape[4] // sources
    order = orders[slot]
    for parity in range(2):
        left = jnp.concatenate([t[parity * half : (parity + 1) * half] for t in turned], axis=0)
        sums = jnp.dot(left, legendre[0, parity], preferred_element_type=jnp.float32)
        degree = 2 * lax.broadcasted_iota(jnp.int32, sums.shape, 1) + parity
        sums = jnp.where(degree >= order, sums, 0.0).astype(jnp.bfloat16)
        for source in range(sources):
            out[0, parity, :, :, source * local : (source + 1) * local, :] = sums[
                source * half : (source + 1) * half
            ].reshape(2, batch, local, sums.shape[1])


def kernel_path(field_grid, norm_gain, norm_bias, order_table, legendre):
    batch, local, hemis, cycles, length = field_grid.shape
    n_ord, n_ch = lax.axis_size("ord"), lax.axis_size("ch")
    order_total, slots = order_table.shape[0], legendre.shape[0]
    fields = batch * local
    groups = order_total // GROUP
    tiles = -(-length // LANES)
    steps = cycles // QUAD
    total = n_ord * n_ch
    tables = angle_tables(order_table, length)
    sign = (1 - 2 * (order_table % 2)).astype(jnp.float32).reshape(groups, 1, GROUP, 1)
    signs = jnp.broadcast_to(sign, (groups, 2, GROUP, LANES)).reshape(groups, 2 * GROUP, LANES)
    gain = jnp.broadcast_to(norm_gain[None, :, None], (batch, local, LANES)).reshape(fields, LANES)
    bias = jnp.broadcast_to(norm_bias[None, :, None], (batch, local, LANES)).reshape(fields, LANES)
    vmem = pl.BlockSpec(memory_space=pltpu.VMEM)
    hbm = pl.BlockSpec(memory_space=pltpu.HBM)
    padded = -(-cycles // 8) * 8 * fields
    arrived = pl.pallas_call(
        partial(exchange_kernel, (n_ord, n_ch, hemis * cycles * n_ord * length)),
        out_shape=jax.ShapeDtypeStruct((n_ch, n_ord, steps, QUAD, slots, LANES), jnp.bfloat16),
        in_specs=[hbm, vmem, vmem, vmem, vmem],
        out_specs=hbm,
        scratch_shapes=[
            pltpu.VMEM((fields, hemis, cycles, length), jnp.bfloat16),
            pltpu.VMEM((hemis, tiles, padded, LANES), jnp.float32),
            pltpu.VMEM((hemis * LANES, tiles * LANES), jnp.bfloat16),
            pltpu.VMEM((groups, 2 * GROUP, tiles * LANES), jnp.bfloat16),
            pltpu.VMEM((total, steps, QUAD, slots, LANES), jnp.bfloat16),
            pltpu.VMEM((2 * fields, LANES), jnp.float32),
            pltpu.VMEM((n_ord, 2 * fields, LANES), jnp.float32),
            pltpu.VMEM((3, fields, LANES), jnp.float32),
            pltpu.SemaphoreType.DMA((8,)),
            pltpu.SemaphoreType.DMA((n_ord,)),
            pltpu.SemaphoreType.DMA((n_ord,)),
            pltpu.SemaphoreType.DMA((total,)),
            pltpu.SemaphoreType.DMA((total,)),
            pltpu.SemaphoreType.DMA,
        ],
        compiler_params=pltpu.CompilerParams(
            collective_id=0, has_side_effects=True, vmem_limit_bytes=60 * 2**20
        ),
        name="spectral_exchange",
    )(field_grid.reshape(fields, hemis, cycles, length), tables, signs, gain, bias)
    depth = n_ord * cycles
    arrived = arrived.reshape(n_ch, depth * slots, LANES)
    own = lax.axis_index("ord") * n_ch + lax.axis_index("ch")
    own_orders = lax.dynamic_slice_in_dim(order_table, own * slots, slots)
    half_degrees = legendre.shape[3]
    return pl.pallas_call(
        legendre_kernel,
        grid=(slots,),
        out_shape=jax.ShapeDtypeStruct((slots, 2, 2, batch, n_ch * local, half_degrees), jnp.bfloat16),
        in_specs=[
            pl.BlockSpec(memory_space=pltpu.SMEM),
            pl.BlockSpec((n_ch, depth * slots, LANES), lambda s: (0, 0, 0)),
            pl.BlockSpec((1, 2, depth, half_degrees), lambda s: (s, 0, 0, 0)),
        ],
        out_specs=pl.BlockSpec(
            (1, 2, 2, batch, n_ch * local, half_degrees), lambda s: (s, 0, 0, 0, 0, 0)
        ),
        scratch_shapes=[pltpu.VMEM((n_ch, depth * slots, LANES), jnp.float32)],
        compiler_params=pltpu.CompilerParams(vmem_limit_bytes=60 * 2**20),
        name="legendre_sums",
    )(own_orders, arrived, legendre)


def on_device(field_grid, norm_gain, norm_bias, order_table, legendre):
    batch, local, hemis, cycles, _ = field_grid.shape
    fits = (
        batch * local * QUAD == LANES
        and hemis == 2
        and cycles % QUAD == 0
        and legendre.shape[0] == 16
        and order_table.shape[0] % GROUP == 0
    )
    path = kernel_path if fits else general_path
    return path(field_grid, norm_gain, norm_bias, order_table, legendre)


def solution(mesh):
    placed = (
        P(None, "ch", None, "ord", None),
        P("ch"),
        P("ch"),
        P(),
        P(("ord", "ch"), None, None, None),
    )
    return jax.shard_map(
        on_device,
        mesh=mesh,
        in_specs=placed,
        out_specs=P(("ord", "ch"), None, None, None, None, None),
        check_vma=False,
    )
```

```python
from functools import partial
import math

import jax
import jax.numpy as jnp
from jax import lax
from jax.experimental import pallas as pl
from jax.experimental.pallas import tpu as pltpu
from jax.sharding import PartitionSpec as P

MESH = pl.DeviceIdType.MESH
LANES = 128
GROUP = 128
QUAD = 4
PITCH = 40


def slot_table(orders, length):
    sample = jnp.arange(length, dtype=jnp.int32)
    phases = sample[:, None] * orders[None, :] % length
    angles = phases.astype(jnp.float32) * (2.0 * math.pi / length)
    factor = 1.0 / math.sqrt(length)
    stacked = jnp.stack([jnp.cos(angles) * factor, -jnp.sin(angles) * factor], axis=2)
    return stacked.reshape(length, 2 * orders.shape[0]).astype(jnp.bfloat16)


def legendre_sums(arrived, legendre, orders):
    odd_order = orders % 2 == 1
    swapped = jnp.where(
        odd_order[:, None, None, None, None, None], arrived[:, :, :, :, ::-1], arrived
    )
    raw_sums = jnp.einsum(
        "srbcpi,spij->sprbcj", swapped, legendre, preferred_element_type=jnp.float32
    )
    half_degrees = legendre.shape[3]
    degree = (
        2 * jnp.arange(half_degrees, dtype=jnp.int32)[None, :]
        + jnp.arange(2, dtype=jnp.int32)[:, None]
    )
    allowed = degree[None, :, :] >= orders[:, None, None]
    return jnp.where(allowed[:, :, None, None, None, :], raw_sums, 0.0).astype(jnp.bfloat16)


def general_path(field_grid, norm_gain, norm_bias, order_table, legendre):
    batch_size, chan_local, hemis, cycle_local, longitudes = field_grid.shape
    order_total = order_table.shape[0]
    values = field_grid.astype(jnp.float32)
    cell_count = hemis * cycle_local * lax.axis_size("ord") * longitudes
    partial_sum = jnp.sum(values, axis=(2, 3, 4))
    totals, squares = lax.psum((partial_sum, jnp.sum(values * values, axis=(2, 3, 4))), "ord")
    average = totals / cell_count
    spread = squares / cell_count - average * average
    centered = values - average[:, :, None, None, None]
    inverse_scale = lax.rsqrt(spread + 1e-05) * norm_gain[None, :]
    normed = (
        centered * inverse_scale[:, :, None, None, None] + norm_bias[None, :, None, None, None]
    ).astype(jnp.bfloat16)
    twiddle = slot_table(order_table, longitudes)
    flat_rows = normed.reshape(-1, longitudes)
    fourier = lax.dot_general(
        twiddle, flat_rows, (((0,), (1,)), ((), ())), preferred_element_type=jnp.float32
    )
    fourier = fourier.reshape(order_total, 2, batch_size, chan_local, hemis, cycle_local)
    north = fourier[:, :, :, :, 0]
    south = fourier[:, :, :, :, 1]
    halves = jnp.stack([north + south, north - south], axis=4).astype(jnp.bfloat16)
    slot_count = legendre.shape[0]
    channel_groups = lax.axis_size("ch")
    first_slot = (lax.axis_index("ord") * channel_groups + lax.axis_index("ch")) * slot_count
    own_orders = lax.dynamic_slice_in_dim(order_table, first_slot, slot_count)
    transform = partial(legendre_sums, legendre=legendre, orders=own_orders)
    arrived = lax.all_to_all(
        lax.all_to_all(halves, "ord", split_axis=0, concat_axis=5, tiled=True),
        "ch",
        split_axis=0,
        concat_axis=3,
        tiled=True,
    )
    return transform(arrived)


def angle_tables(orders, length):
    factor = 1.0 / math.sqrt(length)
    step = 2.0 * math.pi / length
    column = jnp.arange(LANES, dtype=jnp.int32)
    fine = orders[:, None] * column[None, :] % length
    jumps = jnp.where(column == LANES - 1, length // 2, LANES * column)
    coarse = orders[:, None] * jumps[None, :] % length
    fine = fine.astype(jnp.float32) * step
    coarse = coarse.astype(jnp.float32) * step
    return jnp.stack([jnp.cos(fine) * factor, jnp.sin(fine) * factor, jnp.cos(coarse), jnp.sin(coarse)])


def exchange_kernel(
    sizes, orders, field, tables, affine, legendre, out,
    grid, rows, packed, twiddle, signs, sending, arrived, weights, wide, results, stats, stats_in, norms,
    field_sem, stats_out_sem, stats_in_sem, send_sem, recv_sem, own_sem, weight_sem, out_sem,
):
    n_ord, n_ch, cell_count = sizes
    total = n_ord * n_ch
    fields, hemis, cycles, length = grid.shape
    groups = twiddle.shape[0]
    steps = packed.shape[0]
    per_phase = legendre.shape[0] // groups
    tiles = rows.shape[1]
    own_ord, own_ch = lax.axis_index("ord"), lax.axis_index("ch")
    me = own_ord * n_ch + own_ch
    parts = field_sem.shape[0]
    per_part = fields // parts

    def load(part):
        span = pl.ds(part * per_part, per_part)
        return pltpu.make_async_copy(field.at[span], grid.at[span], field_sem.at[part])

    for part in range(parts):
        load(part).start()
    weight_load = pltpu.make_async_copy(legendre, weights, weight_sem)

    barrier = pltpu.get_barrier_semaphore()

    def greet(hop, carry):
        peer = lax.rem(me + hop, total)
        pl.semaphore_signal(
            barrier, inc=1, device_id=(peer // n_ch, lax.rem(peer, n_ch)), device_id_type=MESH
        )
        return carry

    lax.fori_loop(1, total, greet, 0)

    def fold(values):
        summed = values[:, :LANES]
        for tile in range(1, tiles - 1):
            summed += values[:, tile * LANES : (tile + 1) * LANES]
        rest = values[:, (tiles - 1) * LANES :]
        blank = jnp.zeros((1, LANES - rest.shape[1]), jnp.float32)
        return summed + jnp.concatenate([rest, blank], axis=1)

    for part in range(parts):
        load(part).wait()
        if part == parts - 1:
            weight_load.start()

        def measure(at, carry, part=part):
            row = part * per_part + at
            first = grid[row, 0].astype(jnp.float32)
            second = grid[row, 1].astype(jnp.float32)
            stats[pl.ds(row, 1), :] = fold(jnp.sum(first + second, axis=0, keepdims=True))
            stats[pl.ds(fields + row, 1), :] = fold(
                jnp.sum(first * first + second * second, axis=0, keepdims=True)
            )
            return carry

        lax.fori_loop(0, per_part, measure, 0)

    pl.semaphore_wait(barrier, total - 1)

    def stats_copy(hop):
        peer = lax.rem(own_ord + hop, n_ord)
        return pltpu.make_async_remote_copy(
            src_ref=stats,
            dst_ref=stats_in.at[own_ord],
            send_sem=stats_out_sem.at[hop],
            recv_sem=stats_in_sem.at[own_ord],
            device_id=(peer, own_ch),
            device_id_type=MESH,
        )

    for hop in range(1, n_ord):
        stats_copy(hop).start()
    stats_in[own_ord] = stats[...]

    def build(group, carry):
        span = pl.ds(pl.multiple_of(group * GROUP, GROUP), GROUP)
        cos_fine, sin_fine = tables[0, span, :], tables[1, span, :]
        cos_coarse, sin_coarse = tables[2, span, :], tables[3, span, :]
        sign = jnp.where(cos_coarse[:, LANES - 1 :] < 0.0, -1.0, 1.0)
        signs[group] = jnp.broadcast_to(sign, (GROUP, LANES))
        for tile in range(tiles):
            columns = slice(tile * LANES, (tile + 1) * LANES)
            cos_at, sin_at = cos_coarse[:, tile : tile + 1], sin_coarse[:, tile : tile + 1]
            twiddle[group, :GROUP, columns] = (cos_at * cos_fine - sin_at * sin_fine).astype(jnp.bfloat16)
            twiddle[group, GROUP:, columns] = (-(sin_at * cos_fine + cos_at * sin_fine)).astype(jnp.bfloat16)
        return carry

    lax.fori_loop(0, groups, build, 0)

    for hop in range(1, n_ord):
        peer = lax.rem(own_ord + hop, n_ord)
        pltpu.make_async_remote_copy(
            src_ref=stats, dst_ref=stats_in.at[peer], send_sem=stats_out_sem.at[hop],
            recv_sem=stats_in_sem.at[peer], device_id=(peer, own_ch), device_id_type=MESH,
        ).wait()

    merged = stats_in[0]
    for source in range(1, n_ord):
        merged = merged + stats_in[source]
    merged = jnp.sum(merged, axis=1, keepdims=True)
    average = merged[:fields] / cell_count
    spread = merged[fields:] / cell_count - average * average
    scale = lax.rsqrt(spread + 1e-05) * affine[0, :, :1]
    norms[0] = jnp.broadcast_to(average, (fields, LANES))
    norms[1] = jnp.broadcast_to(scale, (fields, LANES))
    norms[2] = affine[1]

    def normalize(at, carry, begin, count):
        shift = norms[0, pl.ds(at, 1), :]
        factor = norms[1, pl.ds(at, 1), :]
        offset = norms[2, pl.ds(at, 1), :]
        for hemi in range(hemis):
            for tile in range(tiles):
                piece = grid[at, hemi, begin : begin + count, tile * LANES : min((tile + 1) * LANES, length)]
                across = piece.shape[1]
                piece = (piece.astype(jnp.float32) - shift[:, :across]) * factor[:, :across] + offset[:, :across]
                if across < LANES:
                    piece = jnp.concatenate([piece, jnp.zeros((count, LANES - across), jnp.float32)], axis=1)
                rows[hemi, tile, pl.ds(at, count, stride=PITCH), :] = piece
        return carry

    lane = lax.broadcasted_iota(jnp.int32, (GROUP, LANES), 1)
    low = lane // fields % 2 == 0
    high = lane // (2 * fields) % 2 == 0

    def swap(mask, upper, lower, amount):
        return (
            jnp.where(mask, upper, pltpu.roll(lower, amount, 1)),
            jnp.where(mask, pltpu.roll(upper, LANES - amount, 1), lower),
        )

    sub = lax.broadcasted_iota(jnp.int32, (GROUP // 8, 8, LANES), 1)
    top = sub < per_phase

    def weave(first, second):
        first, second = first.reshape(GROUP // 8, 8, LANES), second.reshape(GROUP // 8, 8, LANES)
        return (
            jnp.where(top, first, pltpu.roll(second, per_phase, 1)),
            jnp.where(top, pltpu.roll(first, per_phase, 1), second),
        )

    def transform(phase, step):
        spectrum = lax.dot_general(
            twiddle[phase], packed[step], (((1,), (1,)), ((), ())), preferred_element_type=jnp.float32
        )
        sign = signs[phase]
        sign = jnp.concatenate([sign, sign], axis=0)
        north, south = spectrum[:, :LANES], spectrum[:, LANES:] * sign
        even, odd = north + south, north - south
        a, b, c, d = even[:GROUP], even[GROUP:], odd[:GROUP], odd[GROUP:]
        a, b = swap(low, a, b, fields)
        c, d = swap(low, c, d, fields)
        a, c = swap(high, a, c, 2 * fields)
        b, d = swap(high, b, d, 2 * fields)
        front, back = weave(a, b), weave(c, d)
        for side in range(2):
            both = jnp.concatenate([front[side], back[side]], axis=1)
            sending[phase, :, side, step] = both.astype(jnp.bfloat16)

        def send(hop, inner):
            ring = lax.rem(own_ch + hop // n_ord + n_ch // 2, n_ch)
            side = lax.rem(own_ord + hop, n_ord)
            peer = side * n_ch + ring
            pltpu.make_async_remote_copy(
                src_ref=sending.at[phase, peer // 2, lax.rem(peer, 2), step],
                dst_ref=arrived.at[phase, own_ch, own_ord, step],
                send_sem=send_sem.at[phase, peer],
                recv_sem=recv_sem.at[phase, me],
                device_id=(side, ring),
                device_id_type=MESH,
            ).start()
            return inner

        lone = n_ch // 2 * n_ord
        lax.fori_loop(0, lone, send, 0)
        lax.fori_loop(lone + 1, total, send, 0)

    for begin in range(0, cycles, 16):
        count = min(16, cycles - begin)

        lax.fori_loop(0, fields, partial(normalize, begin=begin, count=count), 0)

        def prepare(at, carry, begin=begin):
            step = begin // QUAD + at
            for hemi in range(hemis):
                for quarter in range(QUAD):
                    span = pl.ds(pl.multiple_of((at * QUAD + quarter) * PITCH, 8), fields)
                    place = hemi * LANES + quarter * fields
                    for tile in range(tiles):
                        packed[step, place : place + fields, tile * LANES : (tile + 1) * LANES] = rows[
                            hemi, tile, span, :
                        ].astype(jnp.bfloat16)
            transform(0, step)
            return carry

        lax.fori_loop(0, count // QUAD, prepare, 0)

    def rest(at, carry):
        transform(1 + at // steps, lax.rem(at, steps))
        return carry

    lax.fori_loop(0, (groups - 1) * steps, rest, 0)

    def own_copy(phase):
        return pltpu.make_async_copy(
            sending.at[phase, me // 2, lax.rem(me, 2)], arrived.at[phase, own_ch, own_ord], own_sem.at[phase]
        )

    def out_copy(phase):
        return pltpu.make_async_copy(
            results.at[lax.rem(phase, 2)], out.at[pl.ds(phase * per_phase, per_phase)], out_sem.at[phase]
        )

    for phase in range(groups):
        own_copy(phase).start()
    weight_load.wait()
    batch, local = results.shape[4], results.shape[5] // n_ch
    half = LANES // 2
    depth = n_ord * cycles

    def conclude(phase, carry):
        def finish(hop, inner):
            peer = lax.rem(me + hop, total)
            pltpu.make_async_remote_copy(
                src_ref=sending.at[phase, peer // 2, lax.rem(peer, 2)],
                dst_ref=arrived.at[phase, lax.rem(peer, n_ch), peer // n_ch],
                send_sem=send_sem.at[phase, peer],
                recv_sem=recv_sem.at[phase, peer],
                device_id=(peer // n_ch, lax.rem(peer, n_ch)),
                device_id_type=MESH,
            ).wait()
            return inner

        lax.fori_loop(1, total, finish, 0)
        own_copy(phase).wait()

        @pl.when(phase >= 2)
        def _():
            out_copy(phase - 2).wait()

        for source in range(n_ch):
            wide[source] = arrived[phase, source].astype(jnp.float32).reshape(depth * per_phase, LANES)

        def analyze(at, inner):
            slot = phase * per_phase + at
            order = orders[me * legendre.shape[0] + slot]
            turned = [
                wide[source, pl.ds(at, depth, stride=per_phase), :].T.astype(jnp.bfloat16)
                for source in range(n_ch)
            ]
            for parity in range(2):
                left = jnp.concatenate([t[parity * half : (parity + 1) * half] for t in turned], axis=0)
                sums = jnp.dot(left, weights[slot, parity], preferred_element_type=jnp.float32)
                degree = 2 * lax.broadcasted_iota(jnp.int32, sums.shape, 1) + parity
                sums = jnp.where(degree >= order, sums, 0.0).astype(jnp.bfloat16)
                for source in range(n_ch):
                    results[lax.rem(phase, 2), at, parity, :, :, source * local : (source + 1) * local, :] = sums[
                        source * half : (source + 1) * half
                    ].reshape(2, batch, local, sums.shape[1])
            return inner

        lax.fori_loop(0, per_phase, analyze, 0)
        out_copy(phase).start()
        return carry

    lax.fori_loop(0, groups, conclude, 0)
    for phase in range(groups - 2, groups):
        out_copy(phase).wait()


def kernel_path(field_grid, norm_gain, norm_bias, order_table, legendre):
    batch, local, hemis, cycles, length = field_grid.shape
    n_ord, n_ch = lax.axis_size("ord"), lax.axis_size("ch")
    order_total, slots = order_table.shape[0], legendre.shape[0]
    fields = batch * local
    groups = order_total // GROUP
    tiles = -(-length // LANES)
    steps = cycles // QUAD
    total = n_ord * n_ch
    per_phase = slots // groups
    half_degrees = legendre.shape[3]
    phased = order_table.reshape(total, groups, per_phase).swapaxes(0, 1).reshape(order_total)
    tables = angle_tables(phased, length)
    affine = jnp.stack([norm_gain, norm_bias])[:, None, :, None]
    affine = jnp.broadcast_to(affine, (2, batch, local, LANES)).reshape(2, fields, LANES)
    vmem = pl.BlockSpec(memory_space=pltpu.VMEM)
    hbm = pl.BlockSpec(memory_space=pltpu.HBM)
    depth = n_ord * cycles
    result = (2, 2, batch, n_ch * local, half_degrees)
    return pl.pallas_call(
        partial(exchange_kernel, (n_ord, n_ch, hemis * cycles * n_ord * length)),
        out_shape=jax.ShapeDtypeStruct((slots,) + result, jnp.bfloat16),
        in_specs=[pl.BlockSpec(memory_space=pltpu.SMEM), hbm, vmem, vmem, hbm],
        out_specs=hbm,
        scratch_shapes=[
            pltpu.VMEM((fields, hemis, cycles, length), jnp.bfloat16),
            pltpu.VMEM((hemis, tiles, 16 * PITCH, LANES), jnp.float32),
            pltpu.VMEM((steps, hemis * LANES, tiles * LANES), jnp.bfloat16),
            pltpu.VMEM((groups, 2 * GROUP, tiles * LANES), jnp.bfloat16),
            pltpu.VMEM((groups, GROUP, LANES), jnp.float32),
            pltpu.VMEM((groups, total // 2, 2, steps, QUAD * per_phase, LANES), jnp.bfloat16),
            pltpu.VMEM((groups, n_ch, n_ord, steps, QUAD * per_phase, LANES), jnp.bfloat16),
            pltpu.VMEM(legendre.shape, jnp.bfloat16),
            pltpu.VMEM((n_ch, depth * per_phase, LANES), jnp.float32),
            pltpu.VMEM((2, per_phase) + result, jnp.bfloat16),
            pltpu.VMEM((2 * fields, LANES), jnp.float32),
            pltpu.VMEM((n_ord, 2 * fields, LANES), jnp.float32),
            pltpu.VMEM((3, fields, LANES), jnp.float32),
            pltpu.SemaphoreType.DMA((8,)),
            pltpu.SemaphoreType.DMA((n_ord,)),
            pltpu.SemaphoreType.DMA((n_ord,)),
            pltpu.SemaphoreType.DMA((groups, total)),
            pltpu.SemaphoreType.DMA((groups, total)),
            pltpu.SemaphoreType.DMA((groups,)),
            pltpu.SemaphoreType.DMA,
            pltpu.SemaphoreType.DMA((groups,)),
        ],
        compiler_params=pltpu.CompilerParams(
            collective_id=0, has_side_effects=True, vmem_limit_bytes=63 * 2**20
        ),
        name="spectral_analysis",
    )(order_table, field_grid.reshape(fields, hemis, cycles, length), tables, affine, legendre)


def on_device(field_grid, norm_gain, norm_bias, order_table, legendre):
    batch, local, hemis, cycles, _ = field_grid.shape
    fits = (
        batch * local * QUAD == LANES
        and hemis == 2
        and cycles % QUAD == 0
        and legendre.shape[0] == 16
        and order_table.shape[0] == 4 * GROUP
        and field_grid.shape[4] <= LANES * (LANES - 1)
        and field_grid.shape[4] % 2 == 0
    )
    path = kernel_path if fits else general_path
    return path(field_grid, norm_gain, norm_bias, order_table, legendre)


def solution(mesh):
    placed = (
        P(None, "ch", None, "ord", None),
        P("ch"),
        P("ch"),
        P(),
        P(("ord", "ch"), None, None, None),
    )
    return jax.shard_map(
        on_device,
        mesh=mesh,
        in_specs=placed,
        out_specs=P(("ord", "ch"), None, None, None, None, None),
        check_vma=False,
    )
```

```python
from functools import partial
import math

import jax
import jax.numpy as jnp
from jax import lax
from jax.experimental import pallas as pl
from jax.experimental.pallas import tpu as pltpu
from jax.sharding import PartitionSpec as P

MESH = pl.DeviceIdType.MESH
LANES = 128
GROUP = 128
QUAD = 4
PITCH = 40


def slot_table(orders, length):
    sample = jnp.arange(length, dtype=jnp.int32)
    phases = sample[:, None] * orders[None, :] % length
    angles = phases.astype(jnp.float32) * (2.0 * math.pi / length)
    factor = 1.0 / math.sqrt(length)
    stacked = jnp.stack([jnp.cos(angles) * factor, -jnp.sin(angles) * factor], axis=2)
    return stacked.reshape(length, 2 * orders.shape[0]).astype(jnp.bfloat16)


def legendre_sums(arrived, legendre, orders):
    odd_order = orders % 2 == 1
    swapped = jnp.where(
        odd_order[:, None, None, None, None, None], arrived[:, :, :, :, ::-1], arrived
    )
    raw_sums = jnp.einsum(
        "srbcpi,spij->sprbcj", swapped, legendre, preferred_element_type=jnp.float32
    )
    half_degrees = legendre.shape[3]
    degree = (
        2 * jnp.arange(half_degrees, dtype=jnp.int32)[None, :]
        + jnp.arange(2, dtype=jnp.int32)[:, None]
    )
    allowed = degree[None, :, :] >= orders[:, None, None]
    return jnp.where(allowed[:, :, None, None, None, :], raw_sums, 0.0).astype(jnp.bfloat16)


def general_path(field_grid, norm_gain, norm_bias, order_table, legendre):
    batch_size, chan_local, hemis, cycle_local, longitudes = field_grid.shape
    order_total = order_table.shape[0]
    values = field_grid.astype(jnp.float32)
    cell_count = hemis * cycle_local * lax.axis_size("ord") * longitudes
    partial_sum = jnp.sum(values, axis=(2, 3, 4))
    totals, squares = lax.psum((partial_sum, jnp.sum(values * values, axis=(2, 3, 4))), "ord")
    average = totals / cell_count
    spread = squares / cell_count - average * average
    centered = values - average[:, :, None, None, None]
    inverse_scale = lax.rsqrt(spread + 1e-05) * norm_gain[None, :]
    normed = (
        centered * inverse_scale[:, :, None, None, None] + norm_bias[None, :, None, None, None]
    ).astype(jnp.bfloat16)
    twiddle = slot_table(order_table, longitudes)
    flat_rows = normed.reshape(-1, longitudes)
    fourier = lax.dot_general(
        twiddle, flat_rows, (((0,), (1,)), ((), ())), preferred_element_type=jnp.float32
    )
    fourier = fourier.reshape(order_total, 2, batch_size, chan_local, hemis, cycle_local)
    north = fourier[:, :, :, :, 0]
    south = fourier[:, :, :, :, 1]
    halves = jnp.stack([north + south, north - south], axis=4).astype(jnp.bfloat16)
    slot_count = legendre.shape[0]
    channel_groups = lax.axis_size("ch")
    first_slot = (lax.axis_index("ord") * channel_groups + lax.axis_index("ch")) * slot_count
    own_orders = lax.dynamic_slice_in_dim(order_table, first_slot, slot_count)
    transform = partial(legendre_sums, legendre=legendre, orders=own_orders)
    arrived = lax.all_to_all(
        lax.all_to_all(halves, "ord", split_axis=0, concat_axis=5, tiled=True),
        "ch",
        split_axis=0,
        concat_axis=3,
        tiled=True,
    )
    return transform(arrived)


def angle_tables(orders, length):
    factor = 1.0 / math.sqrt(length)
    step = 2.0 * math.pi / length
    column = jnp.arange(LANES, dtype=jnp.int32)
    fine = orders[:, None] * column[None, :] % length
    jumps = jnp.where(column == LANES - 1, length // 2, LANES * column)
    coarse = orders[:, None] * jumps[None, :] % length
    fine = fine.astype(jnp.float32) * step
    coarse = coarse.astype(jnp.float32) * step
    return jnp.cos(fine) * factor, jnp.sin(fine) * factor, jnp.cos(coarse), jnp.sin(coarse)


def exchange_kernel(
    sizes, orders, field, cos_fines, sin_fines, cos_coarses, sin_coarses, affine, legendre, out,
    grid, rows, packed, twiddle, signs, sending, arrived, weights, wide, results, stats, stats_in, norms,
    field_sem, stats_out_sem, stats_in_sem, send_sem, recv_sem, own_sem, weight_sem, out_sem,
):
    n_ord, n_ch, cell_count = sizes
    total = n_ord * n_ch
    fields, hemis, cycles, length = grid.shape
    groups = twiddle.shape[0]
    steps = packed.shape[0]
    per_phase = legendre.shape[0] // groups
    tiles = rows.shape[1]
    own_ord, own_ch = lax.axis_index("ord"), lax.axis_index("ch")
    me = own_ord * n_ch + own_ch
    parts = field_sem.shape[0]
    per_part = fields // parts

    def load(part):
        span = pl.ds(part * per_part, per_part)
        return pltpu.make_async_copy(field.at[span], grid.at[span], field_sem.at[part])

    for part in range(parts):
        load(part).start()
    weight_load = pltpu.make_async_copy(legendre, weights, weight_sem)

    barrier = pltpu.get_barrier_semaphore()

    def greet(hop, carry):
        peer = lax.rem(me + hop, total)
        pl.semaphore_signal(
            barrier, inc=1, device_id=(peer // n_ch, lax.rem(peer, n_ch)), device_id_type=MESH
        )
        return carry

    lax.fori_loop(1, total, greet, 0)

    def fold(values):
        summed = values[:, :LANES]
        for tile in range(1, tiles - 1):
            summed += values[:, tile * LANES : (tile + 1) * LANES]
        rest = values[:, (tiles - 1) * LANES :]
        blank = jnp.zeros((1, LANES - rest.shape[1]), jnp.float32)
        return summed + jnp.concatenate([rest, blank], axis=1)

    for part in range(parts):
        load(part).wait()
        if part == parts - 1:
            weight_load.start()

        def measure(at, carry, part=part):
            row = part * per_part + at
            first = grid[row, 0].astype(jnp.float32)
            second = grid[row, 1].astype(jnp.float32)
            stats[pl.ds(row, 1), :] = fold(jnp.sum(first + second, axis=0, keepdims=True))
            stats[pl.ds(fields + row, 1), :] = fold(
                jnp.sum(first * first + second * second, axis=0, keepdims=True)
            )
            return carry

        lax.fori_loop(0, per_part, measure, 0)

    pl.semaphore_wait(barrier, total - 1)

    def stats_copy(hop):
        peer = lax.rem(own_ord + hop, n_ord)
        return pltpu.make_async_remote_copy(
            src_ref=stats,
            dst_ref=stats_in.at[own_ord],
            send_sem=stats_out_sem.at[hop],
            recv_sem=stats_in_sem.at[own_ord],
            device_id=(peer, own_ch),
            device_id_type=MESH,
        )

    for hop in range(1, n_ord):
        stats_copy(hop).start()
    stats_in[own_ord] = stats[...]

    def build(group, carry):
        span = pl.ds(pl.multiple_of(group * GROUP, GROUP), GROUP)
        cos_fine, sin_fine = cos_fines[span, :], sin_fines[span, :]
        cos_coarse, sin_coarse = cos_coarses[span, :], sin_coarses[span, :]
        sign = jnp.where(cos_coarse[:, LANES - 1 :] < 0.0, -1.0, 1.0)
        signs[group] = jnp.broadcast_to(sign, (GROUP, LANES))
        for tile in range(tiles):
            columns = slice(tile * LANES, (tile + 1) * LANES)
            cos_at, sin_at = cos_coarse[:, tile : tile + 1], sin_coarse[:, tile : tile + 1]
            twiddle[group, :GROUP, columns] = (cos_at * cos_fine - sin_at * sin_fine).astype(jnp.bfloat16)
            twiddle[group, GROUP:, columns] = (-(sin_at * cos_fine + cos_at * sin_fine)).astype(jnp.bfloat16)
        return carry

    build(0, 0)

    for hop in range(1, n_ord):
        peer = lax.rem(own_ord + hop, n_ord)
        pltpu.make_async_remote_copy(
            src_ref=stats, dst_ref=stats_in.at[peer], send_sem=stats_out_sem.at[hop],
            recv_sem=stats_in_sem.at[peer], device_id=(peer, own_ch), device_id_type=MESH,
        ).wait()

    merged = stats_in[0]
    for source in range(1, n_ord):
        merged = merged + stats_in[source]
    merged = jnp.sum(merged, axis=1, keepdims=True)
    average = merged[:fields] / cell_count
    spread = merged[fields:] / cell_count - average * average
    scale = lax.rsqrt(spread + 1e-05) * affine[0, :, :1]
    norms[0] = jnp.broadcast_to(average, (fields, LANES))
    norms[1] = jnp.broadcast_to(scale, (fields, LANES))
    norms[2] = affine[1]

    def normalize(at, carry, begin, count):
        shift = norms[0, pl.ds(at, 1), :]
        factor = norms[1, pl.ds(at, 1), :]
        offset = norms[2, pl.ds(at, 1), :]
        for hemi in range(hemis):
            for tile in range(tiles):
                piece = grid[at, hemi, begin : begin + count, tile * LANES : min((tile + 1) * LANES, length)]
                across = piece.shape[1]
                piece = (piece.astype(jnp.float32) - shift[:, :across]) * factor[:, :across] + offset[:, :across]
                if across < LANES:
                    piece = jnp.concatenate([piece, jnp.zeros((count, LANES - across), jnp.float32)], axis=1)
                rows[hemi, tile, pl.ds(at, count, stride=PITCH), :] = piece
        return carry

    lane = lax.broadcasted_iota(jnp.int32, (GROUP, LANES), 1)
    low = lane // fields % 2 == 0
    high = lane // (2 * fields) % 2 == 0

    def swap(mask, upper, lower, amount):
        return (
            jnp.where(mask, upper, pltpu.roll(lower, amount, 1)),
            jnp.where(mask, pltpu.roll(upper, LANES - amount, 1), lower),
        )

    sub = lax.broadcasted_iota(jnp.int32, (GROUP // 8, 8, LANES), 1)
    top = sub < per_phase

    def weave(first, second):
        first, second = first.reshape(GROUP // 8, 8, LANES), second.reshape(GROUP // 8, 8, LANES)
        return (
            jnp.where(top, first, pltpu.roll(second, per_phase, 1)),
            jnp.where(top, pltpu.roll(first, per_phase, 1), second),
        )

    def transform(phase, step):
        spectrum = lax.dot_general(
            twiddle[phase], packed[step], (((1,), (1,)), ((), ())), preferred_element_type=jnp.float32
        )
        sign = signs[phase]
        sign = jnp.concatenate([sign, sign], axis=0)
        north, south = spectrum[:, :LANES], spectrum[:, LANES:] * sign
        even, odd = north + south, north - south
        a, b, c, d = even[:GROUP], even[GROUP:], odd[:GROUP], odd[GROUP:]
        a, b = swap(low, a, b, fields)
        c, d = swap(low, c, d, fields)
        a, c = swap(high, a, c, 2 * fields)
        b, d = swap(high, b, d, 2 * fields)
        front, back = weave(a, b), weave(c, d)
        for side in range(2):
            both = jnp.concatenate([front[side], back[side]], axis=1)
            sending[phase, :, side, step] = both.astype(jnp.bfloat16)

        def send(hop, inner):
            ring = lax.rem(own_ch + hop // n_ord + n_ch // 2, n_ch)
            side = lax.rem(own_ord + hop, n_ord)
            peer = side * n_ch + ring
            pltpu.make_async_remote_copy(
                src_ref=sending.at[phase, peer // 2, lax.rem(peer, 2), step],
                dst_ref=arrived.at[phase, own_ch, own_ord, step],
                send_sem=send_sem.at[phase, peer],
                recv_sem=recv_sem.at[phase, me],
                device_id=(side, ring),
                device_id_type=MESH,
            ).start()
            return inner

        lone = n_ch // 2 * n_ord
        lax.fori_loop(0, lone, send, 0)
        lax.fori_loop(lone + 1, total, send, 0)

    begin = count = 0
    while begin + count < cycles:
        begin += count
        count = min(16 if begin else 8, cycles - begin)

        lax.fori_loop(0, fields, partial(normalize, begin=begin, count=count), 0)

        def prepare(at, carry, begin=begin):
            step = begin // QUAD + at
            for hemi in range(hemis):
                for quarter in range(QUAD):
                    span = pl.ds(pl.multiple_of((at * QUAD + quarter) * PITCH, 8), fields)
                    place = hemi * LANES + quarter * fields
                    for tile in range(tiles):
                        packed[step, place : place + fields, tile * LANES : (tile + 1) * LANES] = rows[
                            hemi, tile, span, :
                        ].astype(jnp.bfloat16)
            transform(0, step)
            return carry

        lax.fori_loop(0, count // QUAD, prepare, 0)

    lax.fori_loop(1, groups, build, 0)

    def rest(at, carry):
        transform(1 + at // steps, lax.rem(at, steps))
        return carry

    lax.fori_loop(0, (groups - 1) * steps, rest, 0)

    def own_copy(phase):
        return pltpu.make_async_copy(
            sending.at[phase, me // 2, lax.rem(me, 2)], arrived.at[phase, own_ch, own_ord], own_sem.at[phase]
        )

    def out_copy(phase):
        return pltpu.make_async_copy(
            results.at[lax.rem(phase, 2)], out.at[pl.ds(phase * per_phase, per_phase)], out_sem.at[phase]
        )

    for phase in range(groups):
        own_copy(phase).start()
    weight_load.wait()
    batch, local = results.shape[4], results.shape[5] // n_ch
    half = LANES // 2
    depth = n_ord * cycles

    def conclude(phase, carry):
        def finish(hop, inner):
            peer = lax.rem(me + hop, total)
            pltpu.make_async_remote_copy(
                src_ref=sending.at[phase, peer // 2, lax.rem(peer, 2)],
                dst_ref=arrived.at[phase, lax.rem(peer, n_ch), peer // n_ch],
                send_sem=send_sem.at[phase, peer],
                recv_sem=recv_sem.at[phase, peer],
                device_id=(peer // n_ch, lax.rem(peer, n_ch)),
                device_id_type=MESH,
            ).wait()
            return inner

        lax.fori_loop(1, total, finish, 0)
        own_copy(phase).wait()

        @pl.when(phase >= 2)
        def _():
            out_copy(phase - 2).wait()

        for source in range(n_ch):
            wide[source] = arrived[phase, source].astype(jnp.float32).reshape(depth * per_phase, LANES)

        def analyze(at, inner):
            slot = phase * per_phase + at
            order = orders[me * legendre.shape[0] + slot]
            turned = [
                wide[source, pl.ds(at, depth, stride=per_phase), :].T.astype(jnp.bfloat16)
                for source in range(n_ch)
            ]
            for parity in range(2):
                left = jnp.concatenate([t[parity * half : (parity + 1) * half] for t in turned], axis=0)
                sums = jnp.dot(left, weights[slot, parity], preferred_element_type=jnp.float32)
                degree = 2 * lax.broadcasted_iota(jnp.int32, sums.shape, 1) + parity
                sums = jnp.where(degree >= order, sums, 0.0).astype(jnp.bfloat16)
                for source in range(n_ch):
                    results[lax.rem(phase, 2), at, parity, :, :, source * local : (source + 1) * local, :] = sums[
                        source * half : (source + 1) * half
                    ].reshape(2, batch, local, sums.shape[1])
            return inner

        lax.fori_loop(0, per_phase, analyze, 0)
        out_copy(phase).start()
        return carry

    lax.fori_loop(0, groups, conclude, 0)
    for phase in range(groups - 2, groups):
        out_copy(phase).wait()


def kernel_path(field_grid, norm_gain, norm_bias, order_table, legendre):
    batch, local, hemis, cycles, length = field_grid.shape
    n_ord, n_ch = lax.axis_size("ord"), lax.axis_size("ch")
    order_total, slots = order_table.shape[0], legendre.shape[0]
    fields = batch * local
    groups = order_total // GROUP
    tiles = -(-length // LANES)
    steps = cycles // QUAD
    total = n_ord * n_ch
    per_phase = slots // groups
    half_degrees = legendre.shape[3]
    phased = order_table.reshape(total, groups, per_phase).swapaxes(0, 1).reshape(order_total)
    tables = angle_tables(phased, length)
    affine = jnp.stack([norm_gain, norm_bias])[:, None, :, None]
    affine = jnp.broadcast_to(affine, (2, batch, local, LANES)).reshape(2, fields, LANES)
    vmem = pl.BlockSpec(memory_space=pltpu.VMEM)
    hbm = pl.BlockSpec(memory_space=pltpu.HBM)
    depth = n_ord * cycles
    result = (2, 2, batch, n_ch * local, half_degrees)
    return pl.pallas_call(
        partial(exchange_kernel, (n_ord, n_ch, hemis * cycles * n_ord * length)),
        out_shape=jax.ShapeDtypeStruct((slots,) + result, jnp.bfloat16),
        in_specs=[pl.BlockSpec(memory_space=pltpu.SMEM), hbm, vmem, vmem, vmem, vmem, vmem, hbm],
        out_specs=hbm,
        scratch_shapes=[
            pltpu.VMEM((fields, hemis, cycles, length), jnp.bfloat16),
            pltpu.VMEM((hemis, tiles, 16 * PITCH, LANES), jnp.float32),
            pltpu.VMEM((steps, hemis * LANES, tiles * LANES), jnp.bfloat16),
            pltpu.VMEM((groups, 2 * GROUP, tiles * LANES), jnp.bfloat16),
            pltpu.VMEM((groups, GROUP, LANES), jnp.float32),
            pltpu.VMEM((groups, total // 2, 2, steps, QUAD * per_phase, LANES), jnp.bfloat16),
            pltpu.VMEM((groups, n_ch, n_ord, steps, QUAD * per_phase, LANES), jnp.bfloat16),
            pltpu.VMEM(legendre.shape, jnp.bfloat16),
            pltpu.VMEM((n_ch, depth * per_phase, LANES), jnp.float32),
            pltpu.VMEM((2, per_phase) + result, jnp.bfloat16),
            pltpu.VMEM((2 * fields, LANES), jnp.float32),
            pltpu.VMEM((n_ord, 2 * fields, LANES), jnp.float32),
            pltpu.VMEM((3, fields, LANES), jnp.float32),
            pltpu.SemaphoreType.DMA((8,)),
            pltpu.SemaphoreType.DMA((n_ord,)),
            pltpu.SemaphoreType.DMA((n_ord,)),
            pltpu.SemaphoreType.DMA((groups, total)),
            pltpu.SemaphoreType.DMA((groups, total)),
            pltpu.SemaphoreType.DMA((groups,)),
            pltpu.SemaphoreType.DMA,
            pltpu.SemaphoreType.DMA((groups,)),
        ],
        compiler_params=pltpu.CompilerParams(
            collective_id=0, has_side_effects=True, vmem_limit_bytes=63 * 2**20
        ),
        name="spectral_analysis",
    )(order_table, field_grid.reshape(fields, hemis, cycles, length), *tables, affine, legendre)


def on_device(field_grid, norm_gain, norm_bias, order_table, legendre):
    batch, local, hemis, cycles, _ = field_grid.shape
    fits = (
        batch * local * QUAD == LANES
        and hemis == 2
        and cycles % QUAD == 0
        and legendre.shape[0] == 16
        and order_table.shape[0] == 4 * GROUP
        and field_grid.shape[4] <= LANES * (LANES - 1)
        and field_grid.shape[4] % 2 == 0
    )
    path = kernel_path if fits else general_path
    return path(field_grid, norm_gain, norm_bias, order_table, legendre)


def solution(mesh):
    placed = (
        P(None, "ch", None, "ord", None),
        P("ch"),
        P("ch"),
        P(),
        P(("ord", "ch"), None, None, None),
    )
    return jax.shard_map(
        on_device,
        mesh=mesh,
        in_specs=placed,
        out_specs=P(("ord", "ch"), None, None, None, None, None),
        check_vma=False,
    )
```

```python
from functools import partial
import math

import jax
import jax.numpy as jnp
from jax import lax
from jax.experimental import pallas as pl
from jax.experimental.pallas import tpu as pltpu
from jax.sharding import PartitionSpec as P

MESH = pl.DeviceIdType.MESH
LANES = 128
GROUP = 128
QUAD = 4
PITCH = 40


def slot_table(orders, length):
    sample = jnp.arange(length, dtype=jnp.int32)
    phases = sample[:, None] * orders[None, :] % length
    angles = phases.astype(jnp.float32) * (2.0 * math.pi / length)
    factor = 1.0 / math.sqrt(length)
    stacked = jnp.stack([jnp.cos(angles) * factor, -jnp.sin(angles) * factor], axis=2)
    return stacked.reshape(length, 2 * orders.shape[0]).astype(jnp.bfloat16)


def legendre_sums(arrived, legendre, orders):
    odd_order = orders % 2 == 1
    swapped = jnp.where(
        odd_order[:, None, None, None, None, None], arrived[:, :, :, :, ::-1], arrived
    )
    raw_sums = jnp.einsum(
        "srbcpi,spij->sprbcj", swapped, legendre, preferred_element_type=jnp.float32
    )
    half_degrees = legendre.shape[3]
    degree = (
        2 * jnp.arange(half_degrees, dtype=jnp.int32)[None, :]
        + jnp.arange(2, dtype=jnp.int32)[:, None]
    )
    allowed = degree[None, :, :] >= orders[:, None, None]
    return jnp.where(allowed[:, :, None, None, None, :], raw_sums, 0.0).astype(jnp.bfloat16)


def general_path(field_grid, norm_gain, norm_bias, order_table, legendre):
    batch_size, chan_local, hemis, cycle_local, longitudes = field_grid.shape
    order_total = order_table.shape[0]
    values = field_grid.astype(jnp.float32)
    cell_count = hemis * cycle_local * lax.axis_size("ord") * longitudes
    partial_sum = jnp.sum(values, axis=(2, 3, 4))
    totals, squares = lax.psum((partial_sum, jnp.sum(values * values, axis=(2, 3, 4))), "ord")
    average = totals / cell_count
    spread = squares / cell_count - average * average
    centered = values - average[:, :, None, None, None]
    inverse_scale = lax.rsqrt(spread + 1e-05) * norm_gain[None, :]
    normed = (
        centered * inverse_scale[:, :, None, None, None] + norm_bias[None, :, None, None, None]
    ).astype(jnp.bfloat16)
    twiddle = slot_table(order_table, longitudes)
    flat_rows = normed.reshape(-1, longitudes)
    fourier = lax.dot_general(
        twiddle, flat_rows, (((0,), (1,)), ((), ())), preferred_element_type=jnp.float32
    )
    fourier = fourier.reshape(order_total, 2, batch_size, chan_local, hemis, cycle_local)
    north = fourier[:, :, :, :, 0]
    south = fourier[:, :, :, :, 1]
    halves = jnp.stack([north + south, north - south], axis=4).astype(jnp.bfloat16)
    slot_count = legendre.shape[0]
    channel_groups = lax.axis_size("ch")
    first_slot = (lax.axis_index("ord") * channel_groups + lax.axis_index("ch")) * slot_count
    own_orders = lax.dynamic_slice_in_dim(order_table, first_slot, slot_count)
    transform = partial(legendre_sums, legendre=legendre, orders=own_orders)
    arrived = lax.all_to_all(
        lax.all_to_all(halves, "ord", split_axis=0, concat_axis=5, tiled=True),
        "ch",
        split_axis=0,
        concat_axis=3,
        tiled=True,
    )
    return transform(arrived)


def angle_tables(orders, length):
    factor = 1.0 / math.sqrt(length)
    step = 2.0 * math.pi / length
    column = jnp.arange(LANES, dtype=jnp.int32)
    fine = orders[:, None] * column[None, :] % length
    jumps = jnp.where(column == LANES - 1, length // 2, LANES * column)
    coarse = orders[:, None] * jumps[None, :] % length
    fine = fine.astype(jnp.float32) * step
    coarse = coarse.astype(jnp.float32) * step
    return jnp.cos(fine) * factor, jnp.sin(fine) * factor, jnp.cos(coarse), jnp.sin(coarse)


def exchange_kernel(
    sizes, orders, field, cos_fines, sin_fines, cos_coarses, sin_coarses, affine, legendre, out,
    grid, rows, packed, twiddle, signs, sending, arrived, weights, wide, results, stats, stats_in, norms,
    field_sem, stats_out_sem, stats_in_sem, send_sem, recv_sem, own_sem, weight_sem, out_sem,
):
    n_ord, n_ch, cell_count = sizes
    total = n_ord * n_ch
    fields, hemis, cycles, length = grid.shape
    groups = twiddle.shape[0]
    steps = packed.shape[0]
    per_phase = legendre.shape[0] // groups
    tiles = rows.shape[1]
    own_ord, own_ch = lax.axis_index("ord"), lax.axis_index("ch")
    me = own_ord * n_ch + own_ch
    parts = field_sem.shape[0]
    per_part = fields // parts

    def load(part):
        span = pl.ds(part * per_part, per_part)
        return pltpu.make_async_copy(field.at[span], grid.at[span], field_sem.at[part])

    for part in range(parts):
        load(part).start()
    weight_load = pltpu.make_async_copy(legendre, weights, weight_sem)

    barrier = pltpu.get_barrier_semaphore()

    def greet(hop, carry):
        peer = lax.rem(me + hop, total)
        pl.semaphore_signal(
            barrier, inc=1, device_id=(peer // n_ch, lax.rem(peer, n_ch)), device_id_type=MESH
        )
        return carry

    lax.fori_loop(1, total, greet, 0)

    def fold(values):
        summed = values[:, :LANES]
        for tile in range(1, tiles - 1):
            summed += values[:, tile * LANES : (tile + 1) * LANES]
        rest = values[:, (tiles - 1) * LANES :]
        blank = jnp.zeros((1, LANES - rest.shape[1]), jnp.float32)
        return summed + jnp.concatenate([rest, blank], axis=1)

    for part in range(parts):
        load(part).wait()
        if part == parts - 1:
            weight_load.start()

        def measure(at, carry, part=part):
            row = part * per_part + at
            first = grid[row, 0].astype(jnp.float32)
            second = grid[row, 1].astype(jnp.float32)
            stats[pl.ds(row, 1), :] = fold(jnp.sum(first + second, axis=0, keepdims=True))
            stats[pl.ds(fields + row, 1), :] = fold(
                jnp.sum(first * first + second * second, axis=0, keepdims=True)
            )
            return carry

        lax.fori_loop(0, per_part, measure, 0)

    pl.semaphore_wait(barrier, total - 1)

    def stats_copy(hop):
        peer = lax.rem(own_ord + hop, n_ord)
        return pltpu.make_async_remote_copy(
            src_ref=stats,
            dst_ref=stats_in.at[own_ord],
            send_sem=stats_out_sem.at[hop],
            recv_sem=stats_in_sem.at[own_ord],
            device_id=(peer, own_ch),
            device_id_type=MESH,
        )

    for hop in range(1, n_ord):
        stats_copy(hop).start()
    stats_in[own_ord] = stats[...]

    def build(group, carry):
        span = pl.ds(pl.multiple_of(group * GROUP, GROUP), GROUP)
        cos_fine, sin_fine = cos_fines[span, :], sin_fines[span, :]
        cos_coarse, sin_coarse = cos_coarses[span, :], sin_coarses[span, :]
        sign = jnp.where(cos_coarse[:, LANES - 1 :] < 0.0, -1.0, 1.0)
        signs[group] = jnp.broadcast_to(sign, (GROUP, LANES))
        for tile in range(tiles):
            columns = slice(tile * LANES, (tile + 1) * LANES)
            cos_at, sin_at = cos_coarse[:, tile : tile + 1], sin_coarse[:, tile : tile + 1]
            twiddle[group, :GROUP, columns] = (cos_at * cos_fine - sin_at * sin_fine).astype(jnp.bfloat16)
            twiddle[group, GROUP:, columns] = (-(sin_at * cos_fine + cos_at * sin_fine)).astype(jnp.bfloat16)
        return carry

    build(0, 0)

    for hop in range(1, n_ord):
        peer = lax.rem(own_ord + hop, n_ord)
        pltpu.make_async_remote_copy(
            src_ref=stats, dst_ref=stats_in.at[peer], send_sem=stats_out_sem.at[hop],
            recv_sem=stats_in_sem.at[peer], device_id=(peer, own_ch), device_id_type=MESH,
        ).wait()

    merged = stats_in[0]
    for source in range(1, n_ord):
        merged = merged + stats_in[source]
    merged = jnp.sum(merged, axis=1, keepdims=True)
    average = merged[:fields] / cell_count
    spread = merged[fields:] / cell_count - average * average
    scale = lax.rsqrt(spread + 1e-05) * affine[0, :, :1]
    norms[0] = jnp.broadcast_to(average, (fields, LANES))
    norms[1] = jnp.broadcast_to(scale, (fields, LANES))
    norms[2] = affine[1]

    def normalize(at, carry, begin, count):
        shift = norms[0, pl.ds(at, 1), :]
        factor = norms[1, pl.ds(at, 1), :]
        offset = norms[2, pl.ds(at, 1), :]
        for hemi in range(hemis):
            for tile in range(tiles):
                piece = grid[at, hemi, begin : begin + count, tile * LANES : min((tile + 1) * LANES, length)]
                across = piece.shape[1]
                piece = (piece.astype(jnp.float32) - shift[:, :across]) * factor[:, :across] + offset[:, :across]
                if across < LANES:
                    piece = jnp.concatenate([piece, jnp.zeros((count, LANES - across), jnp.float32)], axis=1)
                rows[hemi, tile, pl.ds(at, count, stride=PITCH), :] = piece
        return carry

    lane = lax.broadcasted_iota(jnp.int32, (GROUP, LANES), 1)
    low = lane // fields % 2 == 0
    high = lane // (2 * fields) % 2 == 0

    def swap(mask, upper, lower, amount):
        return (
            jnp.where(mask, upper, pltpu.roll(lower, amount, 1)),
            jnp.where(mask, pltpu.roll(upper, LANES - amount, 1), lower),
        )

    sub = lax.broadcasted_iota(jnp.int32, (GROUP // 8, 8, LANES), 1)
    top = sub < per_phase

    def weave(first, second):
        first, second = first.reshape(GROUP // 8, 8, LANES), second.reshape(GROUP // 8, 8, LANES)
        return (
            jnp.where(top, first, pltpu.roll(second, per_phase, 1)),
            jnp.where(top, pltpu.roll(first, per_phase, 1), second),
        )

    def transform(phase, step):
        spectrum = lax.dot_general(
            twiddle[phase], packed[step], (((1,), (1,)), ((), ())), preferred_element_type=jnp.float32
        )
        sign = signs[phase]
        sign = jnp.concatenate([sign, sign], axis=0)
        north, south = spectrum[:, :LANES], spectrum[:, LANES:] * sign
        even, odd = north + south, north - south
        a, b, c, d = even[:GROUP], even[GROUP:], odd[:GROUP], odd[GROUP:]
        a, b = swap(low, a, b, fields)
        c, d = swap(low, c, d, fields)
        a, c = swap(high, a, c, 2 * fields)
        b, d = swap(high, b, d, 2 * fields)
        front, back = weave(a, b), weave(c, d)
        for side in range(2):
            both = jnp.concatenate([front[side], back[side]], axis=1)
            sending[phase, :, side, step] = both.astype(jnp.bfloat16)

        def send(hop, inner):
            ring = lax.rem(own_ch + hop // n_ord + n_ch // 2, n_ch)
            side = lax.rem(own_ord + hop, n_ord)
            peer = side * n_ch + ring
            pltpu.make_async_remote_copy(
                src_ref=sending.at[phase, peer // 2, lax.rem(peer, 2), step],
                dst_ref=arrived.at[phase, own_ch, own_ord, step],
                send_sem=send_sem.at[phase, peer],
                recv_sem=recv_sem.at[phase, me],
                device_id=(side, ring),
                device_id_type=MESH,
            ).start()
            return inner

        lone = n_ch // 2 * n_ord
        lax.fori_loop(0, lone, send, 0)
        lax.fori_loop(lone + 1, total, send, 0)

    begin = count = 0
    while begin + count < cycles:
        begin += count
        count = min(16 if begin else 8, cycles - begin)

        lax.fori_loop(0, fields, partial(normalize, begin=begin, count=count), 0)

        def prepare(at, carry, begin=begin):
            step = begin // QUAD + at
            for hemi in range(hemis):
                for quarter in range(QUAD):
                    span = pl.ds(pl.multiple_of((at * QUAD + quarter) * PITCH, 8), fields)
                    place = hemi * LANES + quarter * fields
                    for tile in range(tiles):
                        packed[step, place : place + fields, tile * LANES : (tile + 1) * LANES] = rows[
                            hemi, tile, span, :
                        ].astype(jnp.bfloat16)
            transform(0, step)
            return carry

        lax.fori_loop(0, count // QUAD, prepare, 0)

    lax.fori_loop(1, groups, build, 0)

    def rest(at, carry):
        transform(1 + at // steps, lax.rem(at, steps))
        return carry

    lax.fori_loop(0, (groups - 1) * steps, rest, 0)

    def own_copy(phase):
        return pltpu.make_async_copy(
            sending.at[phase, me // 2, lax.rem(me, 2)], arrived.at[phase, own_ch, own_ord], own_sem.at[phase]
        )

    def out_copy(phase):
        return pltpu.make_async_copy(
            results.at[lax.rem(phase, 2)], out.at[pl.ds(phase * per_phase, per_phase)], out_sem.at[phase]
        )

    for phase in range(groups):
        own_copy(phase).start()
    weight_load.wait()
    batch, local = results.shape[4], results.shape[5] // n_ch
    half = LANES // 2
    depth = n_ord * cycles

    def conclude(phase, carry):
        def finish(hop, inner):
            peer = lax.rem(me + hop, total)
            pltpu.make_async_remote_copy(
                src_ref=sending.at[phase, peer // 2, lax.rem(peer, 2)],
                dst_ref=arrived.at[phase, lax.rem(peer, n_ch), peer // n_ch],
                send_sem=send_sem.at[phase, peer],
                recv_sem=recv_sem.at[phase, peer],
                device_id=(peer // n_ch, lax.rem(peer, n_ch)),
                device_id_type=MESH,
            ).wait()
            return inner

        lax.fori_loop(1, total, finish, 0)
        own_copy(phase).wait()

        @pl.when(phase >= 2)
        def _():
            out_copy(phase - 2).wait()

        for source in range(n_ch):
            wide[source] = arrived[phase, source].astype(jnp.float32).reshape(depth * per_phase, LANES)

        def analyze(at, inner):
            slot = phase * per_phase + at
            order = orders[me * legendre.shape[0] + slot]
            turned = [
                wide[source, pl.ds(at, depth, stride=per_phase), :].T.astype(jnp.bfloat16)
                for source in range(n_ch)
            ]
            for parity in range(2):
                left = jnp.concatenate([t[parity * half : (parity + 1) * half] for t in turned], axis=0)
                sums = jnp.dot(left, weights[slot, parity], preferred_element_type=jnp.float32)
                degree = 2 * lax.broadcasted_iota(jnp.int32, sums.shape, 1) + parity
                sums = jnp.where(degree >= order, sums, 0.0).astype(jnp.bfloat16)
                for source in range(n_ch):
                    results[lax.rem(phase, 2), at, parity, :, :, source * local : (source + 1) * local, :] = sums[
                        source * half : (source + 1) * half
                    ].reshape(2, batch, local, sums.shape[1])
            return inner

        lax.fori_loop(0, per_phase, analyze, 0)
        out_copy(phase).start()
        return carry

    lax.fori_loop(0, groups, conclude, 0)
    for phase in range(groups - 2, groups):
        out_copy(phase).wait()


def emit_kernel(source, target, held, in_sem, out_sem):
    count = held.shape[0]

    def load(at):
        return pltpu.make_async_copy(source.at[at], held.at[at], in_sem.at[at])

    def store(at):
        return pltpu.make_async_copy(held.at[at], target.at[at], out_sem.at[at])

    for at in range(count):
        load(at).start()
    for at in range(count):
        load(at).wait()
        store(at).start()
    for at in range(count):
        store(at).wait()


def kernel_path(field_grid, norm_gain, norm_bias, order_table, legendre):
    batch, local, hemis, cycles, length = field_grid.shape
    n_ord, n_ch = lax.axis_size("ord"), lax.axis_size("ch")
    order_total, slots = order_table.shape[0], legendre.shape[0]
    fields = batch * local
    groups = order_total // GROUP
    tiles = -(-length // LANES)
    steps = cycles // QUAD
    total = n_ord * n_ch
    per_phase = slots // groups
    half_degrees = legendre.shape[3]
    phased = order_table.reshape(total, groups, per_phase).swapaxes(0, 1).reshape(order_total)
    tables = angle_tables(phased, length)
    affine = jnp.stack([norm_gain, norm_bias])[:, None, :, None]
    affine = jnp.broadcast_to(affine, (2, batch, local, LANES)).reshape(2, fields, LANES)
    vmem = pl.BlockSpec(memory_space=pltpu.VMEM)
    hbm = pl.BlockSpec(memory_space=pltpu.HBM)
    depth = n_ord * cycles
    result = (2, 2, batch, n_ch * local, half_degrees)
    summed = pl.pallas_call(
        partial(exchange_kernel, (n_ord, n_ch, hemis * cycles * n_ord * length)),
        out_shape=jax.ShapeDtypeStruct((slots,) + result, jnp.bfloat16),
        in_specs=[pl.BlockSpec(memory_space=pltpu.SMEM), hbm, vmem, vmem, vmem, vmem, vmem, hbm],
        out_specs=hbm,
        scratch_shapes=[
            pltpu.VMEM((fields, hemis, cycles, length), jnp.bfloat16),
            pltpu.VMEM((hemis, tiles, 16 * PITCH, LANES), jnp.float32),
            pltpu.VMEM((steps, hemis * LANES, tiles * LANES), jnp.bfloat16),
            pltpu.VMEM((groups, 2 * GROUP, tiles * LANES), jnp.bfloat16),
            pltpu.VMEM((groups, GROUP, LANES), jnp.float32),
            pltpu.VMEM((groups, total // 2, 2, steps, QUAD * per_phase, LANES), jnp.bfloat16),
            pltpu.VMEM((groups, n_ch, n_ord, steps, QUAD * per_phase, LANES), jnp.bfloat16),
            pltpu.VMEM(legendre.shape, jnp.bfloat16),
            pltpu.VMEM((n_ch, depth * per_phase, LANES), jnp.float32),
            pltpu.VMEM((2, per_phase) + result, jnp.bfloat16),
            pltpu.VMEM((2 * fields, LANES), jnp.float32),
            pltpu.VMEM((n_ord, 2 * fields, LANES), jnp.float32),
            pltpu.VMEM((3, fields, LANES), jnp.float32),
            pltpu.SemaphoreType.DMA((8,)),
            pltpu.SemaphoreType.DMA((n_ord,)),
            pltpu.SemaphoreType.DMA((n_ord,)),
            pltpu.SemaphoreType.DMA((groups, total)),
            pltpu.SemaphoreType.DMA((groups, total)),
            pltpu.SemaphoreType.DMA((groups,)),
            pltpu.SemaphoreType.DMA,
            pltpu.SemaphoreType.DMA((groups,)),
        ],
        compiler_params=pltpu.CompilerParams(
            collective_id=0, has_side_effects=True, vmem_limit_bytes=63 * 2**20
        ),
        name="spectral_analysis",
    )(order_table, field_grid.reshape(fields, hemis, cycles, length), *tables, affine, legendre)
    return pl.pallas_call(
        emit_kernel,
        out_shape=jax.ShapeDtypeStruct(summed.shape, summed.dtype),
        in_specs=[hbm],
        out_specs=hbm,
        scratch_shapes=[
            pltpu.VMEM(summed.shape, summed.dtype),
            pltpu.SemaphoreType.DMA((slots,)),
            pltpu.SemaphoreType.DMA((slots,)),
        ],
        name="emit_result",
    )(summed)


def on_device(field_grid, norm_gain, norm_bias, order_table, legendre):
    batch, local, hemis, cycles, _ = field_grid.shape
    fits = (
        batch * local * QUAD == LANES
        and hemis == 2
        and cycles % QUAD == 0
        and legendre.shape[0] == 16
        and order_table.shape[0] == 4 * GROUP
        and field_grid.shape[4] <= LANES * (LANES - 1)
        and field_grid.shape[4] % 2 == 0
    )
    path = kernel_path if fits else general_path
    return path(field_grid, norm_gain, norm_bias, order_table, legendre)


def solution(mesh):
    placed = (
        P(None, "ch", None, "ord", None),
        P("ch"),
        P("ch"),
        P(),
        P(("ord", "ch"), None, None, None),
    )
    return jax.shard_map(
        on_device,
        mesh=mesh,
        in_specs=placed,
        out_specs=P(("ord", "ch"), None, None, None, None, None),
        check_vma=False,
    )
```
